32 devices in a mesh: dp: 4 (over z), vocab: 8 (over y, x, core).
Axes of the slice: x: 2, y: 2, z: 4, core: 2. Of those that a mesh axis runs over, the one named last changes fastest.
Arguments:
- hidden: bfloat16 [4096, 4096], P(('dp', 'vocab')), may hold values from -4 to 4
- output_weight: bfloat16 [4096, 8192], P(None, 'vocab'), may hold values from -0.09375 to 0.09375
- owners: int32 [4096, 3], P(('dp', 'vocab')), may hold values from 0 to 7, all different within a row; in each aligned block of 128 rows (0 to 127, 128 to 255, ...) at most 64 rows name the same one
- negatives: int32 [4096, 3, 2], P(('dp', 'vocab')), may hold values from 0 to 7
- negative_mask: int32 [4096, 3, 2], P(('dp', 'vocab')), may hold values 0 or 1
- target_block: int32 [4096], P(('dp', 'vocab')), may hold values from 0 to 7
- target_word: int32 [4096], P(('dp', 'vocab')), may hold values from 0 to 127
- log_norm: bfloat16 [4096], P(('dp', 'vocab')), may hold values from 1 to 2
- cotangent: bfloat16 [4096], P(('dp', 'vocab')), may hold values from 4 to 8
Outputs:
- hidden_grad: bfloat16 [4096, 4096], P(('dp', 'vocab'))
- weight_grad: bfloat16 [4096, 8192], P('dp', 'vocab')
The draws below stay inside these ranges and needn't reach their ends.
Inputs may be any that keep to these rules, and one draw needn't show every extreme that they name: Each row names 3 different owners; among the 128 rows of one device no owner is named by more than 64 rows, and in some device's rows an owner is named by exactly 64.
All inputs are finite; a program needn't handle non-finite values. No bound on the sum of `negative_mask` on one device may be relied on, other than what follows from the above.
Results may differ from the reference program's by a relative error of at most 0.015.
Values may be sent and summed in bfloat16 or wider, within the bound.
A program may use at most 128 MiB of HBM per device.

```python
import math
import jax
import jax.numpy as jnp
import numpy as np
from jax import lax

H = 4096
BLOCK = 128
VIS = 3
PER_OWN = 2
BLK_DEV = 8
TOK_DEV = 128
CAP = 64
GROUP_TOK = 1024
TOKENS = 4096
WORDS = 8192
N_DP = 4
N_VOCAB = 8


def set_ends(values, own_key, low, high):
    longest = values.shape.index(max(values.shape))
    spots = []
    for shift in (0, 1):
        where = [jax.random.randint(jax.random.fold_in(own_key, axis), (), 0, length) for axis, length in enumerate(values.shape)]
        where[longest] = (where[longest] + shift) % values.shape[longest]
        spots.append(tuple(where))
    return values.at[spots[0]].set(low).at[spots[1]].set(high)


def block_scale(rng, dims, cuts, least, largest):
    loudness = 1.0
    for position, parts in cuts:
        heights = jax.random.uniform(jax.random.fold_in(jax.random.fold_in(rng, 6), position), (parts,), jnp.float32, least / len(cuts), largest / len(cuts))
        loudness = loudness * jnp.repeat(jnp.exp(heights), dims[position] // parts).reshape((-1,) + (1,) * (len(dims) - 1 - position))
    return loudness


def assign_block(key, own, number, rows, number_of, top, bound, skew):
    sequence = jax.random.permutation(key, number_of)
    crowded, common = load_shares(number_of, rows * top, bound, skew, True), load_shares(number_of, rows * top, bound, skew, False)
    places = jnp.arange(number_of)

    def named(lengths, turn):
        used = int((lengths > 0).sum())
        fixed = max(1, used // 4)
        shifted = fixed + (places - fixed + turn * (used - fixed)) % max(1, number_of - fixed)
        return jnp.zeros((number_of,), jnp.int32).at[sequence[jnp.where(places < fixed, places, shifted)]].set(jnp.asarray(lengths, jnp.int32))

    lengths = jnp.where(number % 4 == 0, named(crowded, number // 4), named(common, number - number // 4 - 1))
    mixed = jax.random.permutation(jax.random.fold_in(own, 3), number_of)
    giver, taker = mixed[0:number_of // 2 * 2:2], mixed[1:number_of // 2 * 2:2]
    slack = jnp.minimum(lengths[giver] - 1, bound - lengths[taker]) // 2
    slack = jnp.where((giver == sequence[0]) | (taker == sequence[0]) | (lengths[taker] == 0), 0, jnp.maximum(slack, 0))
    shifted = jax.random.randint(jax.random.fold_in(own, 4), (number_of // 2,), 0, 1 << 20) % (slack + 1)
    lengths = lengths.at[giver].add(-shifted).at[taker].add(shifted)
    items = jnp.searchsorted(jnp.cumsum(lengths), jnp.arange(rows * top), side="right").astype(jnp.int32)
    table = items.reshape(top, rows).T
    table = table[jax.random.permutation(jax.random.fold_in(own, 1), rows)]
    turn = jax.random.randint(jax.random.fold_in(own, 2), (rows, 1), 0, top)
    return jnp.take_along_axis(table, (jnp.arange(top)[None, :] + turn) % top, axis=1)


def load_shares(number_of, total, bound, slope, full):
    loads = [(1 << 20) // math.isqrt(grade ** slope) + 1 for grade in range(1, number_of + 1)]
    largest = bound if full else min(bound, max(-(-total // number_of), total * loads[0] // sum(loads)))
    least = 1 if total - largest >= number_of - 1 else 0
    counts, surplus = [largest] + [least] * (number_of - 1), total - largest - least * (number_of - 1)
    while surplus > 0:
        candidates = [i for i in range(1, number_of) if counts[i] < largest] or [i for i in range(1, number_of) if counts[i] < bound]
        whole, budget = sum([loads[i] for i in candidates]), surplus
        for i in candidates:
            more = min(bound - counts[i], max(1, budget * loads[i] // whole), surplus)
            counts[i] = counts[i] + more
            surplus = surplus - more
    return np.array(counts)


def scatter_about(rng, shape, spread, most, cuts=(), held_as=jnp.bfloat16):
    values = jax.random.normal(rng, shape, jnp.float32) * spread
    if len(cuts) > 0:
        values = block_scale(rng, shape, cuts, -0.22, 0.18) * values
    return jnp.clip(values, min=-most, max=most).astype(held_as)


def setup_inputs(seed: int = 0) -> dict:
    keys = jax.random.split(jax.random.key(seed), 10)
    hidden = scatter_about(keys[0], (TOKENS, H), 0.5, 4.0, ((0, 32),))
    output_weight = scatter_about(keys[1], (H, WORDS), H ** -0.5, 0.09375, ((1, 8),))
    owners_keys = jax.random.split(jax.random.fold_in(keys[2], 1), TOKENS // TOK_DEV)
    owners_turns = jax.random.permutation(jax.random.fold_in(keys[2], 3), TOKENS // TOK_DEV)
    owners = jax.vmap(lambda own, number: assign_block(jax.random.fold_in(keys[2], 2), own, number, TOK_DEV, N_VOCAB, VIS, CAP, 2))(owners_keys, owners_turns).reshape((TOKENS, VIS))
    negatives = set_ends(jax.random.randint(keys[3], (TOKENS, VIS, PER_OWN), 0, BLK_DEV), jax.random.fold_in(keys[3], 1), 0, BLK_DEV - 1).astype(jnp.int32)
    negative_mask = set_ends((jax.random.randint(keys[4], (TOKENS, VIS, PER_OWN), 0, 4) < 3).astype(jnp.int32), jax.random.fold_in(keys[4], 1), 0, 1)
    target_block = set_ends(jax.random.randint(keys[5], (TOKENS,), 0, BLK_DEV), jax.random.fold_in(keys[5], 1), 0, BLK_DEV - 1).astype(jnp.int32)
    target_word = set_ends(jax.random.randint(keys[6], (TOKENS,), 0, BLOCK), jax.random.fold_in(keys[6], 1), 0, BLOCK - 1).astype(jnp.int32)
    log_norm = jnp.clip(1.0 + 1.0 * jax.random.uniform(keys[7], (TOKENS,), jnp.float32) ** block_scale(keys[7], (TOKENS,), ((0, 32),), -0.2, 0.2), 1.0, 2.0).astype(jnp.bfloat16)
    cotangent = jnp.clip(4.0 + 4.0 * jax.random.uniform(keys[8], (TOKENS,), jnp.float32) ** block_scale(keys[8], (TOKENS,), ((0, 32),), -0.2, 0.2), 4.0, 8.0).astype(jnp.bfloat16)
    return dict(hidden=hidden, output_weight=output_weight, owners=owners, negatives=negatives, negative_mask=negative_mask, target_block=target_block, target_word=target_word, log_norm=log_norm, cotangent=cotangent)


def reference(hidden, output_weight, owners, negatives, negative_mask, target_block, target_word, log_norm, cotangent):
    owner_words = BLK_DEV * BLOCK
    entries = GROUP_TOK * VIS
    reach = N_VOCAB * CAP
    word_position = jnp.arange(owner_words).astype(jnp.float32)
    cluster_ids = jnp.arange(BLK_DEV).astype(jnp.int32)

    def group_step(weight_acc, group):
        first_row = group * GROUP_TOK

        def take_group(array):
            return lax.dynamic_slice_in_dim(array, first_row, GROUP_TOK, 0)

        group_hidden = take_group(hidden)
        flat_owner = take_group(owners).reshape(entries)
        group_negative = take_group(negatives).reshape(entries, PER_OWN)
        group_mask = take_group(negative_mask).reshape(entries, PER_OWN)
        group_block = take_group(target_block)
        group_word = take_group(target_word)
        group_norm = take_group(log_norm)
        group_cotangent = take_group(cotangent)

        def owner_step(owner):
            chosen = jnp.nonzero(flat_owner == owner, size=reach, fill_value=entries)[0].astype(jnp.int32)
            valid = chosen < entries
            safe_index = jnp.minimum(chosen, entries - 1)
            token_of = safe_index // VIS
            is_first = (safe_index % VIS) == 0
            token_rows = jnp.where(valid[:, None], group_hidden[token_of], 0).astype(jnp.bfloat16)
            columns = lax.dynamic_slice_in_dim(output_weight, owner * owner_words, owner_words, 1)
            scores = jnp.dot(token_rows, columns, preferred_element_type=jnp.float32)
            picked_negative = group_negative[safe_index]
            picked_mask = group_mask[safe_index]
            target_here = jnp.where(is_first, group_block[token_of], -1)
            matched = (picked_negative[:, :, None] == cluster_ids[None, None, :]) & (picked_mask[:, :, None] == 1)
            cluster_counts = jnp.sum(jnp.where(matched, 1.0, 0.0), axis=1) + jnp.where(target_here[:, None] == cluster_ids[None, :], 1.0, 0.0)
            word_counts = jnp.repeat(cluster_counts, BLOCK, axis=1)
            target_col = (target_here * BLOCK + group_word[token_of]).astype(jnp.float32)
            token_weight = jnp.where(valid, group_cotangent[token_of].astype(jnp.float32), 0.0)
            log_total = group_norm[token_of].astype(jnp.float32)
            target_hot = jnp.where(word_position[None, :] == target_col[:, None], 1.0, 0.0)
            score_grad = (token_weight[:, None] * (word_counts * jnp.exp(scores - log_total[:, None]) - target_hot)).astype(jnp.bfloat16)
            grad_rows = jnp.dot(score_grad, columns.T, preferred_element_type=jnp.float32).astype(jnp.bfloat16)
            weight_part = jnp.dot(token_rows.T, score_grad, preferred_element_type=jnp.float32).astype(jnp.bfloat16)
            return grad_rows, chosen, weight_part

        grad_rows, chosen, weight_part = lax.map(owner_step, jnp.arange(N_VOCAB).astype(jnp.int32))
        per_entry = jnp.zeros((entries, H), jnp.float32).at[chosen.reshape(-1)].set(grad_rows.reshape(-1, H).astype(jnp.float32), mode="drop")
        hidden_group = jnp.sum(per_entry.reshape(GROUP_TOK, VIS, H), axis=1).astype(jnp.bfloat16)
        weight_acc = weight_acc + jnp.moveaxis(weight_part, 0, 1).reshape(H, N_VOCAB * owner_words).astype(jnp.float32)
        return weight_acc, hidden_group

    weight_acc, hidden_parts = lax.scan(group_step, jnp.zeros((H, WORDS), jnp.float32), jnp.arange(N_DP).astype(jnp.int32))
    return hidden_parts.reshape(TOKENS, H), weight_acc.astype(jnp.bfloat16)
```

```python
import jax
import jax.numpy as jnp
from jax import lax
from jax.sharding import PartitionSpec as P

BLOCK = 128
BLK_DEV = 8
F32 = jnp.float32
BF16 = jnp.bfloat16


def body(
    hidden,
    output_weight,
    owners,
    negatives,
    negative_mask,
    target_block,
    target_word,
    log_norm,
    cotangent,
):
    tokens, width = hidden.shape
    visits = owners.shape[1]
    per_own = negatives.shape[2]
    n_vocab = lax.axis_size("vocab")
    n_dp = lax.axis_size("dp")
    me = lax.axis_index("vocab")
    my_dp = lax.axis_index("dp")
    words = output_weight.shape[1]
    capacity = max(2, tokens * visits * 4 // (3 * n_vocab))
    slots = n_vocab * capacity
    part = width // n_dp

    facts = jnp.concatenate(
        [
            owners.T,
            negatives.reshape(tokens, -1).T,
            negative_mask.reshape(tokens, -1).T,
            target_block[None, :],
            target_word[None, :],
        ],
        axis=0,
    ).astype(BF16)
    facts = jnp.concatenate([facts, log_norm[None, :], cotangent[None, :]], axis=0)
    facts = lax.all_gather(facts, ("dp", "vocab"), axis=0, tiled=False)
    blocks = n_dp * n_vocab

    group_rows = lax.all_gather(hidden, "vocab", axis=0, tiled=False)
    part_rows = lax.all_to_all(hidden, "dp", split_axis=1, concat_axis=0, tiled=True)
    part_rows = lax.all_gather(part_rows.reshape(n_dp, tokens, part), "vocab", axis=1)

    f = facts.astype(F32)
    pairs = visits * per_own
    hit = f[:, :visits, :] == me.astype(F32)
    neg = f[:, visits : visits + pairs, :]
    mask = f[:, visits + pairs : visits + 2 * pairs, :]
    base = visits + 2 * pairs
    t_block, t_word, norm, cot = (f[:, base + i, :] for i in range(4))
    named = jnp.any(hit, axis=1)
    cand = [jnp.where(hit[:, 0], t_block + 1.0, 0.0)]
    for n in range(per_own):
        value = jnp.zeros_like(t_block)
        for v in range(visits):
            i = v * per_own + n
            value = jnp.where(hit[:, v] & (mask[:, i] == 1.0), neg[:, i] + 1.0, value)
        cand.append(value)
    only = []
    for k, value in enumerate(cand):
        for earlier in cand[:k]:
            value = jnp.where(value == earlier, 0.0, value)
        only.append(value)
    upper = jnp.triu(jnp.ones((tokens, tokens), BF16), 1)
    rank = jnp.dot(named.astype(BF16), upper, preferred_element_type=F32)
    place = jnp.where(named, rank, -1.0)
    pick = (
        place[:, None, :] == jnp.arange(capacity, dtype=jnp.int32).astype(F32)[None, :, None]
    ).astype(BF16)
    attrs = jnp.stack(cand + only + [t_word, norm, cot], axis=1).astype(BF16)
    slot_facts = jnp.einsum("sct,sat->sca", pick, attrs, preferred_element_type=F32)
    kinds = per_own + 1
    all_only = slot_facts[:, :, kinds : 2 * kinds].reshape(n_dp * slots, kinds)
    mine = lax.dynamic_slice_in_dim(slot_facts, my_dp * n_vocab, n_vocab, 0).reshape(slots, -1)
    my_pick = lax.dynamic_slice_in_dim(pick, my_dp * n_vocab, n_vocab, 0)

    rows = jnp.einsum("sct,sth->sch", my_pick, group_rows, preferred_element_type=F32)
    rows = rows.astype(BF16).reshape(slots, width)
    scores = jnp.dot(rows, output_weight, preferred_element_type=F32)
    word_ids = jnp.arange(words, dtype=jnp.int32)[None, :]
    word_block = (word_ids // BLOCK + 1).astype(F32)
    word_in = (word_ids % BLOCK).astype(F32)
    counts = jnp.zeros((slots, words), F32)
    for k in range(kinds):
        counts = counts + jnp.where(mine[:, k : k + 1] == word_block, 1.0, 0.0)
    hot = jnp.where(
        (mine[:, 0:1] == word_block) & (mine[:, 2 * kinds : 2 * kinds + 1] == word_in), 1.0, 0.0
    )
    norm_col = mine[:, 2 * kinds + 1 : 2 * kinds + 2]
    cot_col = mine[:, 2 * kinds + 2 : 2 * kinds + 3]
    grown = jnp.where(counts > 0.0, counts * jnp.exp(scores - norm_col), 0.0)
    grad = (cot_col * (grown - hot)).astype(BF16)

    packed = []
    for k in range(kinds):
        which = mine[:, kinds + k : kinds + k + 1]
        value = jnp.zeros((slots, BLOCK), BF16)
        for b in range(BLK_DEV):
            value = jnp.where(which == b + 1.0, grad[:, b * BLOCK : (b + 1) * BLOCK], value)
        packed.append(value)
    packed = jnp.concatenate(packed, axis=1)
    packed = lax.all_gather(packed, "dp", axis=0, tiled=True)

    back = lax.dot_general(
        grad, output_weight, (((1,), (1,)), ((), ())), preferred_element_type=F32
    ).astype(BF16)
    back = jnp.einsum(
        "sct,sch->sth", my_pick, back.reshape(n_vocab, capacity, width), preferred_element_type=F32
    ).astype(BF16)
    hidden_grad = lax.psum_scatter(
        back.reshape(n_vocab * tokens, width), "vocab", scatter_dimension=0, tiled=True
    )

    part_slots = jnp.einsum(
        "sct,sth->sch",
        pick,
        part_rows.reshape(blocks, tokens, part),
        preferred_element_type=F32,
    ).astype(BF16).reshape(n_dp * slots, part)
    spread = []
    for b in range(BLK_DEV):
        value = jnp.zeros((n_dp * slots, BLOCK), BF16)
        for k in range(kinds):
            value = jnp.where(
                all_only[:, k : k + 1] == b + 1.0, packed[:, k * BLOCK : (k + 1) * BLOCK], value
            )
        spread.append(value)
    spread = jnp.concatenate(spread, axis=1)
    weight_grad = lax.dot_general(
        part_slots, spread, (((0,), (0,)), ((), ())), preferred_element_type=F32
    ).astype(BF16)
    return (hidden_grad, weight_grad)


def solution(mesh):
    placed = (
        P(("dp", "vocab"), None),
        P(None, "vocab"),
        P(("dp", "vocab"), None),
        P(("dp", "vocab"), None, None),
        P(("dp", "vocab"), None, None),
        P(("dp", "vocab")),
        P(("dp", "vocab")),
        P(("dp", "vocab")),
        P(("dp", "vocab")),
    )
    return jax.shard_map(
        body,
        mesh=mesh,
        in_specs=placed,
        out_specs=(P(("dp", "vocab"), None), P("dp", "vocab")),
        check_vma=False,
    )
```

```python
import jax
import jax.numpy as jnp
from jax import lax
from jax.experimental import pallas as pl
from jax.experimental.pallas import tpu as pltpu
from jax.sharding import PartitionSpec as P

BLOCK = 128
BLK_DEV = 8
F32 = jnp.float32
BF16 = jnp.bfloat16


MESH = pl.DeviceIdType.MESH
CUBE = 8


def cube_peers():
    v = lax.axis_index("vocab")
    core = v % 2
    x = (v // 2) % 2
    y = v // 4
    return v, v + 1 - 2 * core, v + 2 - 4 * x, v + 4 - 8 * y


def greet(vocab_peers, dp_peers):
    barrier = pltpu.get_barrier_semaphore()
    for peer in vocab_peers:
        pl.semaphore_signal(barrier, inc=1, device_id={"vocab": peer}, device_id_type=MESH)
    for peer in dp_peers:
        pl.semaphore_signal(barrier, inc=1, device_id={"dp": peer}, device_id_type=MESH)
    pl.semaphore_wait(barrier, len(vocab_peers) + len(dp_peers))


def front_kernel(n_dp, h_ref, f_ref, g_ref, p_ref, fo_ref, send, recv, local):
    v, sib, xp, yp = cube_peers()
    diag = xp + yp - v
    dp = lax.axis_index("dp")
    tokens, width = h_ref.shape
    part = width // n_dp
    half = tokens // 2
    others = [(v + u) % CUBE for u in range(1, CUBE)]
    groups = [(dp + n_dp - k) % n_dp for k in range(1, n_dp)]
    greet(others, groups)
    used = [0]

    def push(src, dst, **where):
        i = used[0]
        used[0] += 1
        copy = pltpu.make_async_remote_copy(
            src_ref=src,
            dst_ref=dst,
            send_sem=send.at[i],
            recv_sem=recv.at[i],
            device_id=where,
            device_id_type=MESH,
        )
        copy.start()
        copies.append(copy)
        return copy

    copies = []
    low, high = pl.ds(0, half), pl.ds(half, half)
    keep_rows = pltpu.make_async_copy(h_ref, g_ref.at[v], local.at[0])
    keep_rows.start()
    keep_facts = pltpu.make_async_copy(f_ref, fo_ref.at[v, 0], local.at[1])
    keep_facts.start()
    facts_in = [push(f_ref, fo_ref.at[v, k + 1], dp=groups[k]) for k in range(n_dp - 1)]
    x_low = push(h_ref.at[low], g_ref.at[v, low], vocab=xp)
    y_high = push(h_ref.at[high], g_ref.at[v, high], vocab=yp)
    x_high = push(h_ref.at[high], g_ref.at[v, high], vocab=xp)
    y_low = push(h_ref.at[low], g_ref.at[v, low], vocab=yp)
    s_own = push(h_ref, g_ref.at[v], vocab=sib)
    parts_in = []
    for k in range(n_dp - 1):
        columns = pl.ds(pl.multiple_of(groups[k] * part, part), part)
        parts_in.append(push(h_ref.at[:, columns], p_ref.at[k], dp=groups[k]))
    for copy in facts_in:
        copy.wait_recv()
    keep_facts.wait()
    facts_out = [push(fo_ref.at[v], fo_ref.at[v], vocab=peer) for peer in others]
    x_low.wait_recv()
    d_low = push(g_ref.at[xp, low], g_ref.at[xp, low], vocab=yp)
    s1 = push(g_ref.at[xp, low], g_ref.at[xp, low], vocab=sib)
    y_high.wait_recv()
    d_high = push(g_ref.at[yp, high], g_ref.at[yp, high], vocab=xp)
    s2 = push(g_ref.at[yp, high], g_ref.at[yp, high], vocab=sib)
    x_high.wait_recv()
    s3 = push(g_ref.at[xp, high], g_ref.at[xp, high], vocab=sib)
    y_low.wait_recv()
    s4 = push(g_ref.at[yp, low], g_ref.at[yp, low], vocab=sib)
    d_low.wait_recv()
    s5 = push(g_ref.at[diag, low], g_ref.at[diag, low], vocab=sib)
    d_high.wait_recv()
    s6 = push(g_ref.at[diag, high], g_ref.at[diag, high], vocab=sib)
    for copy in [s_own, s1, s2, s3, s4, s5, s6] + parts_in + facts_out:
        copy.wait_recv()
    for copy in copies:
        copy.wait_send()
    keep_rows.wait()


def front(hidden, facts, n_dp):
    tokens, width = hidden.shape
    total = 2 * (n_dp - 1) + 5 + (CUBE - 1) + 8
    return pl.pallas_call(
        lambda *refs: front_kernel(n_dp, *refs),
        out_shape=(
            jax.ShapeDtypeStruct((CUBE, tokens, width), BF16),
            jax.ShapeDtypeStruct((n_dp - 1, tokens, width // n_dp), BF16),
            jax.ShapeDtypeStruct((CUBE, n_dp) + facts.shape, BF16),
        ),
        in_specs=[pl.BlockSpec(memory_space=pltpu.VMEM)] * 2,
        out_specs=(pl.BlockSpec(memory_space=pl.ANY),) * 3,
        scratch_shapes=[
            pltpu.SemaphoreType.DMA((total,)),
            pltpu.SemaphoreType.DMA((total,)),
            pltpu.SemaphoreType.DMA((2,)),
        ],
        compiler_params=pltpu.CompilerParams(collective_id=0, has_side_effects=True),
        name="front",
    )(hidden, facts)


def add_rows(out_ref, first, rows, *parts):
    step = 16

    @pl.loop(0, rows // step)
    def _(i):
        at = pl.ds(pl.multiple_of(first + i * step, step), step)
        total = parts[0](i * step, step).astype(F32)
        for item in parts[1:]:
            total = total + item(i * step, step).astype(F32)
        out_ref[at, :] = total.astype(BF16)


def rows_of(ref, first):
    return lambda start, count: ref[pl.ds(pl.multiple_of(first + start, count), count), :]


def back_kernel(n_dp, b_ref, k_ref, o_ref, ko_ref, sbuf, sums, hx, hy, fx, fy, send, recv, local):
    v, sib, xp, yp = cube_peers()
    diag = xp + yp - v
    shift = sib - v
    dp = lax.axis_index("dp")
    tokens = o_ref.shape[0]
    half = tokens // 2
    groups = [(dp + n_dp - k) % n_dp for k in range(1, n_dp)]
    greet([sib, xp, yp], groups)
    copies = []

    def push(src, dst, **where):
        i = len(copies)
        copy = pltpu.make_async_remote_copy(
            src_ref=src,
            dst_ref=dst,
            send_sem=send.at[i],
            recv_sem=recv.at[i],
            device_id=where,
            device_id_type=MESH,
        )
        copy.start()
        copies.append(copy)
        return copy

    keep = pltpu.make_async_copy(k_ref, ko_ref.at[0], local.at[0])
    keep.start()
    order = [diag, xp, yp, v]
    pair = [push(b_ref.at[q + shift], sbuf.at[i], vocab=sib) for i, q in enumerate(order)]
    packs = [push(k_ref, ko_ref.at[k + 1], dp=groups[k]) for k in range(n_dp - 1)]
    low, high = pl.ds(0, half), pl.ds(half, half)

    def add_pair(i, first):
        add_rows(
            sums.at[i], first, half, rows_of(b_ref.at[order[i]], first), rows_of(sbuf.at[i], first)
        )

    def add_hop(i, first, hop):
        add_rows(
            sums.at[i],
            first,
            half,
            rows_of(b_ref.at[order[i]], first),
            rows_of(sbuf.at[i], first),
            rows_of(hop, 0),
        )

    pair[0].wait_recv()
    add_pair(0, 0)
    to_x = push(sums.at[0, low], hx, vocab=xp)
    add_pair(0, half)
    to_y = push(sums.at[0, high], hy, vocab=yp)
    pair[1].wait_recv()
    add_pair(1, 0)
    x_low = push(sums.at[1, low], fx.at[low], vocab=xp)
    pair[2].wait_recv()
    add_pair(2, half)
    y_high = push(sums.at[2, high], fy.at[high], vocab=yp)
    to_y.wait_recv()
    add_hop(1, half, hy)
    x_high = push(sums.at[1, high], fx.at[high], vocab=xp)
    to_x.wait_recv()
    add_hop(2, 0, hx)
    y_low = push(sums.at[2, low], fy.at[low], vocab=yp)
    pair[3].wait_recv()
    for copy in (x_low, x_high, y_low, y_high):
        copy.wait_recv()
    add_rows(
        o_ref,
        0,
        tokens,
        rows_of(b_ref.at[v], 0),
        rows_of(sbuf.at[3], 0),
        rows_of(fx, 0),
        rows_of(fy, 0),
    )
    for copy in packs:
        copy.wait_recv()
    for copy in copies:
        copy.wait_send()
    keep.wait()


def back_sum(back, packed, n_dp):
    tokens, width = back.shape[1:]
    total = 4 + 6 + n_dp - 1
    vmem = pl.BlockSpec(memory_space=pltpu.VMEM)
    return pl.pallas_call(
        lambda *refs: back_kernel(n_dp, *refs),
        out_shape=(
            jax.ShapeDtypeStruct((tokens, width), BF16),
            jax.ShapeDtypeStruct((n_dp,) + packed.shape, BF16),
        ),
        in_specs=[vmem, vmem],
        out_specs=(vmem, pl.BlockSpec(memory_space=pl.ANY)),
        scratch_shapes=[
            pltpu.VMEM((4, tokens, width), BF16),
            pltpu.VMEM((3, tokens, width), BF16),
            pltpu.VMEM((tokens // 2, width), BF16),
            pltpu.VMEM((tokens // 2, width), BF16),
            pltpu.VMEM((tokens, width), BF16),
            pltpu.VMEM((tokens, width), BF16),
            pltpu.SemaphoreType.DMA((total,)),
            pltpu.SemaphoreType.DMA((total,)),
            pltpu.SemaphoreType.DMA((1,)),
        ],
        compiler_params=pltpu.CompilerParams(collective_id=1, has_side_effects=True),
        name="back_sum",
    )(back, packed)


def body(
    hidden,
    output_weight,
    owners,
    negatives,
    negative_mask,
    target_block,
    target_word,
    log_norm,
    cotangent,
):
    tokens, width = hidden.shape
    visits = owners.shape[1]
    per_own = negatives.shape[2]
    n_vocab = lax.axis_size("vocab")
    n_dp = lax.axis_size("dp")
    me = lax.axis_index("vocab")
    my_dp = lax.axis_index("dp")
    words = output_weight.shape[1]
    capacity = max(2, tokens * visits * 4 // (3 * n_vocab))
    slots = n_vocab * capacity
    part = width // n_dp

    facts = jnp.concatenate(
        [
            owners.T,
            negatives.reshape(tokens, -1).T,
            negative_mask.reshape(tokens, -1).T,
            target_block[None, :],
            target_word[None, :],
        ],
        axis=0,
    ).astype(BF16)
    facts = jnp.concatenate([facts, log_norm[None, :], cotangent[None, :]], axis=0)
    facts = jnp.pad(facts, ((0, -facts.shape[0] % 16), (0, 0)))
    blocks = n_dp * n_vocab

    cube = n_vocab == CUBE
    if cube:
        group_rows, part_rows, facts = front(hidden, facts, n_dp)
    else:
        group_rows = lax.all_gather(hidden, "vocab", axis=0, tiled=False)
        part_rows = lax.all_to_all(hidden, "dp", split_axis=1, concat_axis=0, tiled=True)
        part_rows = jnp.roll(part_rows.reshape(n_dp, tokens, part), -my_dp, axis=0)[1:]
        facts = lax.all_gather(lax.all_gather(facts, "dp", axis=0), "vocab", axis=0)
        facts = jnp.roll(facts, -my_dp, axis=1)
    part_rows = lax.all_gather(part_rows, "vocab", axis=1)
    facts = jnp.swapaxes(facts, 0, 1).reshape(blocks, -1, tokens)

    f = facts.astype(F32)
    pairs = visits * per_own
    hit = f[:, :visits, :] == me.astype(F32)
    neg = f[:, visits : visits + pairs, :]
    mask = f[:, visits + pairs : visits + 2 * pairs, :]
    base = visits + 2 * pairs
    t_block, t_word, norm, cot = (f[:, base + i, :] for i in range(4))
    named = jnp.any(hit, axis=1)
    cand = [jnp.where(hit[:, 0], t_block + 1.0, 0.0)]
    for n in range(per_own):
        value = jnp.zeros_like(t_block)
        for v in range(visits):
            i = v * per_own + n
            value = jnp.where(hit[:, v] & (mask[:, i] == 1.0), neg[:, i] + 1.0, value)
        cand.append(value)
    only = []
    for k, value in enumerate(cand):
        for earlier in cand[:k]:
            value = jnp.where(value == earlier, 0.0, value)
        only.append(value)
    upper = jnp.triu(jnp.ones((tokens, tokens), BF16), 1)
    rank = jnp.dot(named.astype(BF16), upper, preferred_element_type=F32)
    place = jnp.where(named, rank, -1.0)
    pick = (
        place[:, None, :] == jnp.arange(capacity, dtype=jnp.int32).astype(F32)[None, :, None]
    ).astype(BF16)
    attrs = jnp.stack(cand + only + [t_word, norm, cot], axis=1).astype(BF16)
    slot_facts = jnp.einsum("sct,sat->sca", pick, attrs, preferred_element_type=F32)
    kinds = per_own + 1
    all_only = slot_facts[:, :, kinds : 2 * kinds].reshape(n_dp * slots, kinds)
    mine = slot_facts[:n_vocab].reshape(slots, -1)
    my_pick = pick[:n_vocab]

    rows = jnp.einsum("sct,sth->sch", my_pick, group_rows, preferred_element_type=F32)
    rows = rows.astype(BF16).reshape(slots, width)
    scores = jnp.dot(rows, output_weight, preferred_element_type=F32)
    word_ids = jnp.arange(words, dtype=jnp.int32)[None, :]
    word_block = (word_ids // BLOCK + 1).astype(F32)
    word_in = (word_ids % BLOCK).astype(F32)
    counts = jnp.zeros((slots, words), F32)
    for k in range(kinds):
        counts = counts + jnp.where(mine[:, k : k + 1] == word_block, 1.0, 0.0)
    hot = jnp.where(
        (mine[:, 0:1] == word_block) & (mine[:, 2 * kinds : 2 * kinds + 1] == word_in), 1.0, 0.0
    )
    norm_col = mine[:, 2 * kinds + 1 : 2 * kinds + 2]
    cot_col = mine[:, 2 * kinds + 2 : 2 * kinds + 3]
    grown = jnp.where(counts > 0.0, counts * jnp.exp(scores - norm_col), 0.0)
    grad = (cot_col * (grown - hot)).astype(BF16)

    packed = []
    for k in range(kinds):
        which = mine[:, kinds + k : kinds + k + 1]
        value = jnp.zeros((slots, BLOCK), BF16)
        for b in range(BLK_DEV):
            value = jnp.where(which == b + 1.0, grad[:, b * BLOCK : (b + 1) * BLOCK], value)
        packed.append(value)
    packed = jnp.concatenate(packed, axis=1)
    back = lax.dot_general(
        grad, output_weight, (((1,), (1,)), ((), ())), preferred_element_type=F32
    ).astype(BF16)
    back = jnp.einsum(
        "sct,sch->sth", my_pick, back.reshape(n_vocab, capacity, width), preferred_element_type=F32
    ).astype(BF16)
    if cube:
        hidden_grad, packed = back_sum(back, packed, n_dp)
    else:
        hidden_grad = lax.psum_scatter(
            back.reshape(n_vocab * tokens, width), "vocab", scatter_dimension=0, tiled=True
        )
        packed = jnp.roll(lax.all_gather(packed, "dp", axis=0), -my_dp, axis=0)
    packed = packed.reshape(n_dp * slots, kinds * BLOCK)

    part_slots = jnp.einsum(
        "sct,sth->sch",
        pick[n_vocab:],
        part_rows.reshape(blocks - n_vocab, tokens, part),
        preferred_element_type=F32,
    ).astype(BF16).reshape((n_dp - 1) * slots, part)
    own_slots = lax.dynamic_slice_in_dim(rows, my_dp * part, part, 1)
    part_slots = jnp.concatenate([own_slots, part_slots], axis=0)
    spread = []
    for b in range(BLK_DEV):
        value = jnp.zeros((n_dp * slots, BLOCK), BF16)
        for k in range(kinds):
            value = jnp.where(
                all_only[:, k : k + 1] == b + 1.0, packed[:, k * BLOCK : (k + 1) * BLOCK], value
            )
        spread.append(value)
    spread = jnp.concatenate(spread, axis=1)
    weight_grad = lax.dot_general(
        part_slots, spread, (((0,), (0,)), ((), ())), preferred_element_type=F32
    ).astype(BF16)
    return (hidden_grad, weight_grad)


def solution(mesh):
    placed = (
        P(("dp", "vocab"), None),
        P(None, "vocab"),
        P(("dp", "vocab"), None),
        P(("dp", "vocab"), None, None),
        P(("dp", "vocab"), None, None),
        P(("dp", "vocab")),
        P(("dp", "vocab")),
        P(("dp", "vocab")),
        P(("dp", "vocab")),
    )
    return jax.shard_map(
        body,
        mesh=mesh,
        in_specs=placed,
        out_specs=(P(("dp", "vocab"), None), P("dp", "vocab")),
        check_vma=False,
    )
```

```python
import jax
import jax.numpy as jnp
from jax import lax
from jax.experimental import pallas as pl
from jax.experimental.pallas import tpu as pltpu
from jax.sharding import PartitionSpec as P

BLOCK = 128
BLK_DEV = 8
F32 = jnp.float32
BF16 = jnp.bfloat16


MESH = pl.DeviceIdType.MESH
CUBE = 8


def cube_peers():
    v = lax.axis_index("vocab")
    core = v % 2
    x = (v // 2) % 2
    y = v // 4
    return v, v + 1 - 2 * core, v + 2 - 4 * x, v + 4 - 8 * y


def greet(vocab_peers, dp_peers):
    barrier = pltpu.get_barrier_semaphore()
    for peer in vocab_peers:
        pl.semaphore_signal(barrier, inc=1, device_id={"vocab": peer}, device_id_type=MESH)
    for peer in dp_peers:
        pl.semaphore_signal(barrier, inc=1, device_id={"dp": peer}, device_id_type=MESH)
    pl.semaphore_wait(barrier, len(vocab_peers) + len(dp_peers))


def front_kernel(n_dp, h_ref, f_ref, g_ref, p_ref, fo_ref, send, recv, local):
    v, sib, xp, yp = cube_peers()
    diag = xp + yp - v
    dp = lax.axis_index("dp")
    tokens, width = h_ref.shape
    part = width // n_dp
    half = tokens // 2
    others = [(v + u) % CUBE for u in range(1, CUBE)]
    groups = [(dp + n_dp - k) % n_dp for k in range(1, n_dp)]
    greet(others, groups)
    used = [0]

    def push(src, dst, **where):
        i = used[0]
        used[0] += 1
        copy = pltpu.make_async_remote_copy(
            src_ref=src,
            dst_ref=dst,
            send_sem=send.at[i],
            recv_sem=recv.at[i],
            device_id=where,
            device_id_type=MESH,
        )
        copy.start()
        copies.append(copy)
        return copy

    copies = []
    low, high = pl.ds(0, half), pl.ds(half, half)
    keep_rows = pltpu.make_async_copy(h_ref, g_ref.at[v], local.at[0])
    keep_rows.start()
    keep_facts = pltpu.make_async_copy(f_ref, fo_ref.at[v, 0], local.at[1])
    keep_facts.start()
    facts_in = [push(f_ref, fo_ref.at[v, k + 1], dp=groups[k]) for k in range(n_dp - 1)]
    x_low = push(h_ref.at[low], g_ref.at[v, low], vocab=xp)
    y_high = push(h_ref.at[high], g_ref.at[v, high], vocab=yp)
    x_high = push(h_ref.at[high], g_ref.at[v, high], vocab=xp)
    y_low = push(h_ref.at[low], g_ref.at[v, low], vocab=yp)
    s_own = push(h_ref, g_ref.at[v], vocab=sib)
    parts_in = []
    for k in range(n_dp - 1):
        columns = pl.ds(pl.multiple_of(groups[k] * part, part), part)
        parts_in.append(push(h_ref.at[:, columns], p_ref.at[k], dp=groups[k]))
    for copy in facts_in:
        copy.wait_recv()
    keep_facts.wait()
    facts_out = [push(fo_ref.at[v], fo_ref.at[v], vocab=peer) for peer in others]
    x_low.wait_recv()
    d_low = push(g_ref.at[xp, low], g_ref.at[xp, low], vocab=yp)
    s1 = push(g_ref.at[xp, low], g_ref.at[xp, low], vocab=sib)
    y_high.wait_recv()
    d_high = push(g_ref.at[yp, high], g_ref.at[yp, high], vocab=xp)
    s2 = push(g_ref.at[yp, high], g_ref.at[yp, high], vocab=sib)
    x_high.wait_recv()
    s3 = push(g_ref.at[xp, high], g_ref.at[xp, high], vocab=sib)
    y_low.wait_recv()
    s4 = push(g_ref.at[yp, low], g_ref.at[yp, low], vocab=sib)
    d_low.wait_recv()
    s5 = push(g_ref.at[diag, low], g_ref.at[diag, low], vocab=sib)
    d_high.wait_recv()
    s6 = push(g_ref.at[diag, high], g_ref.at[diag, high], vocab=sib)
    for copy in [s_own, s1, s2, s3, s4, s5, s6] + parts_in + facts_out:
        copy.wait_recv()
    for copy in copies:
        copy.wait_send()
    keep_rows.wait()


def front(hidden, facts, n_dp):
    tokens, width = hidden.shape
    total = 2 * (n_dp - 1) + 5 + (CUBE - 1) + 8
    return pl.pallas_call(
        lambda *refs: front_kernel(n_dp, *refs),
        out_shape=(
            jax.ShapeDtypeStruct((CUBE, tokens, width), BF16),
            jax.ShapeDtypeStruct((n_dp - 1, tokens, width // n_dp), BF16),
            jax.ShapeDtypeStruct((CUBE, n_dp) + facts.shape, BF16),
        ),
        in_specs=[pl.BlockSpec(memory_space=pltpu.VMEM)] * 2,
        out_specs=(pl.BlockSpec(memory_space=pl.ANY),) * 3,
        scratch_shapes=[
            pltpu.SemaphoreType.DMA((total,)),
            pltpu.SemaphoreType.DMA((total,)),
            pltpu.SemaphoreType.DMA((2,)),
        ],
        compiler_params=pltpu.CompilerParams(collective_id=0, has_side_effects=True),
        name="front",
    )(hidden, facts)


def add_rows(out_ref, first, rows, *parts):
    step = 16

    @pl.loop(0, rows // step)
    def _(i):
        at = pl.ds(pl.multiple_of(first + i * step, step), step)
        total = parts[0](i * step, step).astype(F32)
        for item in parts[1:]:
            total = total + item(i * step, step).astype(F32)
        out_ref[at, :] = total.astype(BF16)


def rows_of(ref, first):
    return lambda start, count: ref[pl.ds(pl.multiple_of(first + start, count), count), :]


def back_kernel(n_dp, b_ref, k_ref, o_ref, ko_ref, sbuf, sums, hx, hy, fx, fy, send, recv, local):
    v, sib, xp, yp = cube_peers()
    diag = xp + yp - v
    shift = sib - v
    dp = lax.axis_index("dp")
    tokens = o_ref.shape[0]
    half = tokens // 2
    groups = [(dp + n_dp - k) % n_dp for k in range(1, n_dp)]
    greet([sib, xp, yp], groups)
    copies = []

    def push(src, dst, **where):
        i = len(copies)
        copy = pltpu.make_async_remote_copy(
            src_ref=src,
            dst_ref=dst,
            send_sem=send.at[i],
            recv_sem=recv.at[i],
            device_id=where,
            device_id_type=MESH,
        )
        copy.start()
        copies.append(copy)
        return copy

    keep = pltpu.make_async_copy(k_ref, ko_ref.at[0], local.at[0])
    keep.start()
    order = [diag, xp, yp, v]
    pair = [push(b_ref.at[q + shift], sbuf.at[i], vocab=sib) for i, q in enumerate(order)]
    packs = [push(k_ref, ko_ref.at[k + 1], dp=groups[k]) for k in range(n_dp - 1)]
    low, high = pl.ds(0, half), pl.ds(half, half)

    def add_pair(i, first):
        add_rows(
            sums.at[i], first, half, rows_of(b_ref.at[order[i]], first), rows_of(sbuf.at[i], first)
        )

    def add_hop(i, first, hop):
        add_rows(
            sums.at[i],
            first,
            half,
            rows_of(b_ref.at[order[i]], first),
            rows_of(sbuf.at[i], first),
            rows_of(hop, 0),
        )

    pair[0].wait_recv()
    add_pair(0, 0)
    to_x = push(sums.at[0, low], hx, vocab=xp)
    add_pair(0, half)
    to_y = push(sums.at[0, high], hy, vocab=yp)
    pair[1].wait_recv()
    add_pair(1, 0)
    x_low = push(sums.at[1, low], fx.at[low], vocab=xp)
    pair[2].wait_recv()
    add_pair(2, half)
    y_high = push(sums.at[2, high], fy.at[high], vocab=yp)
    to_y.wait_recv()
    add_hop(1, half, hy)
    x_high = push(sums.at[1, high], fx.at[high], vocab=xp)
    to_x.wait_recv()
    add_hop(2, 0, hx)
    y_low = push(sums.at[2, low], fy.at[low], vocab=yp)
    pair[3].wait_recv()
    for copy in (x_low, x_high, y_low, y_high):
        copy.wait_recv()
    add_rows(
        o_ref,
        0,
        tokens,
        rows_of(b_ref.at[v], 0),
        rows_of(sbuf.at[3], 0),
        rows_of(fx, 0),
        rows_of(fy, 0),
    )
    for copy in packs:
        copy.wait_recv()
    for copy in copies:
        copy.wait_send()
    keep.wait()


def back_sum(back, packed, n_dp):
    tokens, width = back.shape[1:]
    total = 4 + 6 + n_dp - 1
    vmem = pl.BlockSpec(memory_space=pltpu.VMEM)
    return pl.pallas_call(
        lambda *refs: back_kernel(n_dp, *refs),
        out_shape=(
            jax.ShapeDtypeStruct((tokens, width), BF16),
            jax.ShapeDtypeStruct((n_dp,) + packed.shape, BF16),
        ),
        in_specs=[vmem, vmem],
        out_specs=(vmem, pl.BlockSpec(memory_space=pl.ANY)),
        scratch_shapes=[
            pltpu.VMEM((4, tokens, width), BF16),
            pltpu.VMEM((3, tokens, width), BF16),
            pltpu.VMEM((tokens // 2, width), BF16),
            pltpu.VMEM((tokens // 2, width), BF16),
            pltpu.VMEM((tokens, width), BF16),
            pltpu.VMEM((tokens, width), BF16),
            pltpu.SemaphoreType.DMA((total,)),
            pltpu.SemaphoreType.DMA((total,)),
            pltpu.SemaphoreType.DMA((1,)),
        ],
        compiler_params=pltpu.CompilerParams(collective_id=1, has_side_effects=True),
        name="back_sum",
    )(back, packed)


def weight_kernel(own_ref, pick_ref, part_ref, packed_ref, only_ref, o_ref, lhs, lhs_t, acc):
    g = pl.program_id(0)
    sources, capacity = pick_ref.shape[:2]
    kinds = only_ref.shape[1]
    pair = 2 * BLOCK

    @pl.when(g == 0)
    def _():
        lhs[...] = own_ref[...]
        acc[...] = jnp.zeros_like(acc)

    @pl.when(g > 0)
    def _():
        for s in range(sources):
            lhs[s * capacity : (s + 1) * capacity, :] = jnp.dot(
                pick_ref[s], part_ref[0, s], preferred_element_type=F32
            ).astype(BF16)

    lhs_t[...] = lhs[...].T

    @pl.loop(0, acc.shape[1] // pair)
    def _(j):
        sides = []
        for i in range(2):
            block = (2 * j + i + 1).astype(F32)
            value = jnp.zeros((lhs.shape[0], BLOCK), F32)
            for k in range(kinds):
                value = jnp.where(
                    only_ref[:, k : k + 1] == block,
                    packed_ref[0, :, k * BLOCK : (k + 1) * BLOCK].astype(F32),
                    value,
                )
            sides.append(value.astype(BF16))
        spread = jnp.concatenate(sides, axis=1)
        at = pl.ds(pl.multiple_of(j * pair, pair), pair)
        acc[:, at] += jnp.dot(lhs_t[...], spread, preferred_element_type=F32)

    @pl.when(g == pl.num_programs(0) - 1)
    def _():
        o_ref[...] = acc[...].astype(BF16)


def weight_product(own, pick, parts, packed, only, words):
    groups, slots = packed.shape[:2]
    _, sources, tokens, part = parts.shape
    capacity = pick.shape[1]
    kinds = only.shape[1]
    return pl.pallas_call(
        weight_kernel,
        grid=(groups,),
        out_shape=jax.ShapeDtypeStruct((part, words), BF16),
        in_specs=[
            pl.BlockSpec((slots, part), lambda g: (0, 0)),
            pl.BlockSpec((sources, capacity, tokens), lambda g: (jnp.maximum(g - 1, 0), 0, 0)),
            pl.BlockSpec((1, sources, tokens, part), lambda g: (jnp.maximum(g - 1, 0), 0, 0, 0)),
            pl.BlockSpec((1, slots, packed.shape[2]), lambda g: (g, 0, 0)),
            pl.BlockSpec((slots, kinds), lambda g: (g, 0)),
        ],
        out_specs=pl.BlockSpec((part, words), lambda g: (0, 0)),
        scratch_shapes=[
            pltpu.VMEM((slots, part), BF16),
            pltpu.VMEM((part, slots), BF16),
            pltpu.VMEM((part, words), F32),
        ],
        compiler_params=pltpu.CompilerParams(dimension_semantics=("arbitrary",)),
        name="weight_product",
    )(own, pick, parts, packed, only)


def body(
    hidden,
    output_weight,
    owners,
    negatives,
    negative_mask,
    target_block,
    target_word,
    log_norm,
    cotangent,
):
    tokens, width = hidden.shape
    visits = owners.shape[1]
    per_own = negatives.shape[2]
    n_vocab = lax.axis_size("vocab")
    n_dp = lax.axis_size("dp")
    me = lax.axis_index("vocab")
    my_dp = lax.axis_index("dp")
    words = output_weight.shape[1]
    capacity = max(2, tokens * visits * 4 // (3 * n_vocab))
    slots = n_vocab * capacity
    part = width // n_dp

    facts = jnp.concatenate(
        [
            owners.T,
            negatives.reshape(tokens, -1).T,
            negative_mask.reshape(tokens, -1).T,
            target_block[None, :],
            target_word[None, :],
        ],
        axis=0,
    ).astype(BF16)
    facts = jnp.concatenate([facts, log_norm[None, :], cotangent[None, :]], axis=0)
    facts = jnp.pad(facts, ((0, -facts.shape[0] % 16), (0, 0)))
    blocks = n_dp * n_vocab

    cube = n_vocab == CUBE
    if cube:
        group_rows, part_rows, facts = front(hidden, facts, n_dp)
    else:
        group_rows = lax.all_gather(hidden, "vocab", axis=0, tiled=False)
        part_rows = lax.all_to_all(hidden, "dp", split_axis=1, concat_axis=0, tiled=True)
        part_rows = jnp.roll(part_rows.reshape(n_dp, tokens, part), -my_dp, axis=0)[1:]
        facts = lax.all_gather(lax.all_gather(facts, "dp", axis=0), "vocab", axis=0)
        facts = jnp.roll(facts, -my_dp, axis=1)
    part_rows = lax.all_gather(part_rows, "vocab", axis=1)
    facts = jnp.swapaxes(facts, 0, 1).reshape(blocks, -1, tokens)

    f = facts.astype(F32)
    pairs = visits * per_own
    hit = f[:, :visits, :] == me.astype(F32)
    neg = f[:, visits : visits + pairs, :]
    mask = f[:, visits + pairs : visits + 2 * pairs, :]
    base = visits + 2 * pairs
    t_block, t_word, norm, cot = (f[:, base + i, :] for i in range(4))
    named = jnp.any(hit, axis=1)
    cand = [jnp.where(hit[:, 0], t_block + 1.0, 0.0)]
    for n in range(per_own):
        value = jnp.zeros_like(t_block)
        for v in range(visits):
            i = v * per_own + n
            value = jnp.where(hit[:, v] & (mask[:, i] == 1.0), neg[:, i] + 1.0, value)
        cand.append(value)
    only = []
    for k, value in enumerate(cand):
        for earlier in cand[:k]:
            value = jnp.where(value == earlier, 0.0, value)
        only.append(value)
    upper = jnp.triu(jnp.ones((tokens, tokens), BF16), 1)
    rank = jnp.dot(named.astype(BF16), upper, preferred_element_type=F32)
    place = jnp.where(named, rank, -1.0)
    pick = (
        place[:, None, :] == jnp.arange(capacity, dtype=jnp.int32).astype(F32)[None, :, None]
    ).astype(BF16)
    attrs = jnp.stack(cand + only + [t_word, norm, cot], axis=1).astype(BF16)
    slot_facts = jnp.einsum("sct,sat->sca", pick, attrs, preferred_element_type=F32)
    kinds = per_own + 1
    all_only = slot_facts[:, :, kinds : 2 * kinds].reshape(n_dp * slots, kinds)
    mine = slot_facts[:n_vocab].reshape(slots, -1)
    my_pick = pick[:n_vocab]

    rows = jnp.einsum("sct,sth->sch", my_pick, group_rows, preferred_element_type=F32)
    rows = rows.astype(BF16).reshape(slots, width)
    scores = jnp.dot(rows, output_weight, preferred_element_type=F32)
    word_ids = jnp.arange(words, dtype=jnp.int32)[None, :]
    word_block = (word_ids // BLOCK + 1).astype(F32)
    word_in = (word_ids % BLOCK).astype(F32)
    counts = jnp.zeros((slots, words), F32)
    for k in range(kinds):
        counts = counts + jnp.where(mine[:, k : k + 1] == word_block, 1.0, 0.0)
    hot = jnp.where(
        (mine[:, 0:1] == word_block) & (mine[:, 2 * kinds : 2 * kinds + 1] == word_in), 1.0, 0.0
    )
    norm_col = mine[:, 2 * kinds + 1 : 2 * kinds + 2]
    cot_col = mine[:, 2 * kinds + 2 : 2 * kinds + 3]
    grown = jnp.where(counts > 0.0, counts * jnp.exp(scores - norm_col), 0.0)
    grad = (cot_col * (grown - hot)).astype(BF16)

    packed = []
    for k in range(kinds):
        which = mine[:, kinds + k : kinds + k + 1]
        value = jnp.zeros((slots, BLOCK), BF16)
        for b in range(BLK_DEV):
            value = jnp.where(which == b + 1.0, grad[:, b * BLOCK : (b + 1) * BLOCK], value)
        packed.append(value)
    packed = jnp.concatenate(packed, axis=1)
    back = lax.dot_general(
        grad, output_weight, (((1,), (1,)), ((), ())), preferred_element_type=F32
    ).astype(BF16)
    back = jnp.einsum(
        "sct,sch->sth", my_pick, back.reshape(n_vocab, capacity, width), preferred_element_type=F32
    ).astype(BF16)
    if cube:
        hidden_grad, packed = back_sum(back, packed, n_dp)
    else:
        hidden_grad = lax.psum_scatter(
            back.reshape(n_vocab * tokens, width), "vocab", scatter_dimension=0, tiled=True
        )
        packed = jnp.roll(lax.all_gather(packed, "dp", axis=0), -my_dp, axis=0)
    own_slots = lax.dynamic_slice_in_dim(rows, my_dp * part, part, 1)
    weight_grad = weight_product(own_slots, pick[n_vocab:], part_rows, packed, all_only, words)
    return (hidden_grad, weight_grad)


def solution(mesh):
    placed = (
        P(("dp", "vocab"), None),
        P(None, "vocab"),
        P(("dp", "vocab"), None),
        P(("dp", "vocab"), None, None),
        P(("dp", "vocab"), None, None),
        P(("dp", "vocab")),
        P(("dp", "vocab")),
        P(("dp", "vocab")),
        P(("dp", "vocab")),
    )
    return jax.shard_map(
        body,
        mesh=mesh,
        in_specs=placed,
        out_specs=(P(("dp", "vocab"), None), P("dp", "vocab")),
        check_vma=False,
    )
```

```python
import jax
import jax.numpy as jnp
from jax import lax
from jax.experimental import pallas as pl
from jax.experimental.pallas import tpu as pltpu
from jax.sharding import PartitionSpec as P

BLOCK = 128
BLK_DEV = 8
F32 = jnp.float32
BF16 = jnp.bfloat16


MESH = pl.DeviceIdType.MESH
CUBE = 8


def cube_peers():
    v = lax.axis_index("vocab")
    core = v % 2
    x = (v // 2) % 2
    y = v // 4
    return v, v + 1 - 2 * core, v + 2 - 4 * x, v + 4 - 8 * y


def greet(vocab_peers, dp_peers):
    barrier = pltpu.get_barrier_semaphore()
    for peer in vocab_peers:
        pl.semaphore_signal(barrier, inc=1, device_id={"vocab": peer}, device_id_type=MESH)
    for peer in dp_peers:
        pl.semaphore_signal(barrier, inc=1, device_id={"dp": peer}, device_id_type=MESH)
    pl.semaphore_wait(barrier, len(vocab_peers) + len(dp_peers))


def front_kernel(n_dp, h_ref, f_ref, g_ref, p_ref, fo_ref, send, recv, local):
    v, sib, xp, yp = cube_peers()
    diag = xp + yp - v
    dp = lax.axis_index("dp")
    tokens, width = h_ref.shape
    part = width // n_dp
    half = tokens // 2
    others = [(v + u) % CUBE for u in range(1, CUBE)]
    groups = [(dp + n_dp - k) % n_dp for k in range(1, n_dp)]
    greet(others, groups)
    used = [0]

    def push(src, dst, **where):
        i = used[0]
        used[0] += 1
        copy = pltpu.make_async_remote_copy(
            src_ref=src,
            dst_ref=dst,
            send_sem=send.at[i],
            recv_sem=recv.at[i],
            device_id=where,
            device_id_type=MESH,
        )
        copy.start()
        copies.append(copy)
        return copy

    copies = []
    low, high = pl.ds(0, half), pl.ds(half, half)
    keep_rows = pltpu.make_async_copy(h_ref, g_ref.at[v], local.at[0])
    keep_rows.start()
    keep_facts = pltpu.make_async_copy(f_ref, fo_ref.at[v, 0], local.at[1])
    keep_facts.start()
    facts_in = [push(f_ref, fo_ref.at[v, k + 1], dp=groups[k]) for k in range(n_dp - 1)]
    x_low = push(h_ref.at[low], g_ref.at[v, low], vocab=xp)
    y_high = push(h_ref.at[high], g_ref.at[v, high], vocab=yp)
    x_high = push(h_ref.at[high], g_ref.at[v, high], vocab=xp)
    y_low = push(h_ref.at[low], g_ref.at[v, low], vocab=yp)
    s_own = push(h_ref, g_ref.at[v], vocab=sib)
    parts_in = []
    for k in range(n_dp - 1):
        columns = pl.ds(pl.multiple_of(groups[k] * part, part), part)
        parts_in.append(push(h_ref.at[:, columns], p_ref.at[k], dp=groups[k]))
    for copy in facts_in:
        copy.wait_recv()
    keep_facts.wait()
    facts_out = [push(fo_ref.at[v], fo_ref.at[v], vocab=peer) for peer in others]
    x_low.wait_recv()
    d_low = push(g_ref.at[xp, low], g_ref.at[xp, low], vocab=yp)
    s1 = push(g_ref.at[xp, low], g_ref.at[xp, low], vocab=sib)
    y_high.wait_recv()
    d_high = push(g_ref.at[yp, high], g_ref.at[yp, high], vocab=xp)
    s2 = push(g_ref.at[yp, high], g_ref.at[yp, high], vocab=sib)
    x_high.wait_recv()
    s3 = push(g_ref.at[xp, high], g_ref.at[xp, high], vocab=sib)
    y_low.wait_recv()
    s4 = push(g_ref.at[yp, low], g_ref.at[yp, low], vocab=sib)
    d_low.wait_recv()
    s5 = push(g_ref.at[diag, low], g_ref.at[diag, low], vocab=sib)
    d_high.wait_recv()
    s6 = push(g_ref.at[diag, high], g_ref.at[diag, high], vocab=sib)
    for copy in [s_own, s1, s2, s3, s4, s5, s6] + parts_in + facts_out:
        copy.wait_recv()
    for copy in copies:
        copy.wait_send()
    keep_rows.wait()


def front(hidden, facts, n_dp):
    tokens, width = hidden.shape
    total = 2 * (n_dp - 1) + 5 + (CUBE - 1) + 8
    return pl.pallas_call(
        lambda *refs: front_kernel(n_dp, *refs),
        out_shape=(
            jax.ShapeDtypeStruct((CUBE, tokens, width), BF16),
            jax.ShapeDtypeStruct((n_dp - 1, tokens, width // n_dp), BF16),
            jax.ShapeDtypeStruct((CUBE, n_dp) + facts.shape, BF16),
        ),
        in_specs=[pl.BlockSpec(memory_space=pltpu.VMEM)] * 2,
        out_specs=(pl.BlockSpec(memory_space=pl.ANY),) * 3,
        scratch_shapes=[
            pltpu.SemaphoreType.DMA((total,)),
            pltpu.SemaphoreType.DMA((total,)),
            pltpu.SemaphoreType.DMA((2,)),
        ],
        compiler_params=pltpu.CompilerParams(collective_id=0, has_side_effects=True),
        name="front",
    )(hidden, facts)


def add_rows(out_ref, first, rows, *parts):
    step = 16

    @pl.loop(0, rows // step)
    def _(i):
        at = pl.ds(pl.multiple_of(first + i * step, step), step)
        total = parts[0](i * step, step).astype(F32)
        for item in parts[1:]:
            total = total + item(i * step, step).astype(F32)
        out_ref[at, :] = total.astype(BF16)


def rows_of(ref, first):
    return lambda start, count: ref[pl.ds(pl.multiple_of(first + start, count), count), :]


def back_kernel(n_dp, b_ref, k_ref, o_ref, ko_ref, sbuf, sums, hx, hy, fx, fy, send, recv, local):
    v, sib, xp, yp = cube_peers()
    diag = xp + yp - v
    shift = sib - v
    dp = lax.axis_index("dp")
    tokens = o_ref.shape[0]
    half = tokens // 2
    groups = [(dp + n_dp - k) % n_dp for k in range(1, n_dp)]
    greet([sib, xp, yp], groups)
    copies = []

    def push(src, dst, **where):
        i = len(copies)
        copy = pltpu.make_async_remote_copy(
            src_ref=src,
            dst_ref=dst,
            send_sem=send.at[i],
            recv_sem=recv.at[i],
            device_id=where,
            device_id_type=MESH,
        )
        copy.start()
        copies.append(copy)
        return copy

    keep = pltpu.make_async_copy(k_ref, ko_ref.at[0], local.at[0])
    keep.start()
    order = [diag, xp, yp, v]
    pair = [push(b_ref.at[q + shift], sbuf.at[i], vocab=sib) for i, q in enumerate(order)]
    packs = [push(k_ref, ko_ref.at[k + 1], dp=groups[k]) for k in range(n_dp - 1)]
    low, high = pl.ds(0, half), pl.ds(half, half)

    def add_pair(i, first):
        add_rows(
            sums.at[i], first, half, rows_of(b_ref.at[order[i]], first), rows_of(sbuf.at[i], first)
        )

    def add_hop(i, first, hop):
        add_rows(
            sums.at[i],
            first,
            half,
            rows_of(b_ref.at[order[i]], first),
            rows_of(sbuf.at[i], first),
            rows_of(hop, 0),
        )

    pair[0].wait_recv()
    add_pair(0, 0)
    to_x = push(sums.at[0, low], hx, vocab=xp)
    add_pair(0, half)
    to_y = push(sums.at[0, high], hy, vocab=yp)
    pair[1].wait_recv()
    add_pair(1, 0)
    x_low = push(sums.at[1, low], fx.at[low], vocab=xp)
    pair[2].wait_recv()
    add_pair(2, half)
    y_high = push(sums.at[2, high], fy.at[high], vocab=yp)
    to_y.wait_recv()
    add_hop(1, half, hy)
    x_high = push(sums.at[1, high], fx.at[high], vocab=xp)
    to_x.wait_recv()
    add_hop(2, 0, hx)
    y_low = push(sums.at[2, low], fy.at[low], vocab=yp)
    pair[3].wait_recv()
    for copy in (x_low, x_high, y_low, y_high):
        copy.wait_recv()
    add_rows(
        o_ref,
        0,
        tokens,
        rows_of(b_ref.at[v], 0),
        rows_of(sbuf.at[3], 0),
        rows_of(fx, 0),
        rows_of(fy, 0),
    )
    for copy in packs:
        copy.wait_recv()
    for copy in copies:
        copy.wait_send()
    keep.wait()


def back_sum(back, packed, n_dp):
    tokens, width = back.shape[1:]
    total = 4 + 6 + n_dp - 1
    vmem = pl.BlockSpec(memory_space=pltpu.VMEM)
    return pl.pallas_call(
        lambda *refs: back_kernel(n_dp, *refs),
        out_shape=(
            jax.ShapeDtypeStruct((tokens, width), BF16),
            jax.ShapeDtypeStruct((n_dp,) + packed.shape, BF16),
        ),
        in_specs=[vmem, vmem],
        out_specs=(vmem, pl.BlockSpec(memory_space=pl.ANY)),
        scratch_shapes=[
            pltpu.VMEM((4, tokens, width), BF16),
            pltpu.VMEM((3, tokens, width), BF16),
            pltpu.VMEM((tokens // 2, width), BF16),
            pltpu.VMEM((tokens // 2, width), BF16),
            pltpu.VMEM((tokens, width), BF16),
            pltpu.VMEM((tokens, width), BF16),
            pltpu.SemaphoreType.DMA((total,)),
            pltpu.SemaphoreType.DMA((total,)),
            pltpu.SemaphoreType.DMA((1,)),
        ],
        compiler_params=pltpu.CompilerParams(collective_id=1, has_side_effects=True),
        name="back_sum",
    )(back, packed)


def weight_kernel(own_ref, pick_ref, part_ref, packed_ref, only_ref, o_ref, lhs, lhs_t, acc):
    g = pl.program_id(0)
    sources, capacity = pick_ref.shape[:2]
    kinds = only_ref.shape[1]
    pair = 2 * BLOCK

    @pl.when(g == 0)
    def _():
        lhs[...] = own_ref[...]
        acc[...] = jnp.zeros_like(acc)

    @pl.when(g > 0)
    def _():
        for s in range(sources):
            lhs[s * capacity : (s + 1) * capacity, :] = jnp.dot(
                pick_ref[s], part_ref[0, s], preferred_element_type=F32
            ).astype(BF16)

    lhs_t[...] = lhs[...].T

    @pl.loop(0, acc.shape[1] // pair, unroll=True)
    def _(j):
        sides = []
        for i in range(2):
            block = (2 * j + i + 1).astype(F32)
            value = jnp.zeros((lhs.shape[0], BLOCK), F32)
            for k in range(kinds):
                value = jnp.where(
                    only_ref[:, k : k + 1] == block,
                    packed_ref[0, :, k * BLOCK : (k + 1) * BLOCK].astype(F32),
                    value,
                )
            sides.append(value.astype(BF16))
        spread = jnp.concatenate(sides, axis=1)
        at = pl.ds(pl.multiple_of(j * pair, pair), pair)
        acc[:, at] += jnp.dot(lhs_t[...], spread, preferred_element_type=F32)

    @pl.when(g == pl.num_programs(0) - 1)
    def _():
        o_ref[...] = acc[...].astype(BF16)


def weight_product(own, pick, parts, packed, only, words):
    groups, slots = packed.shape[:2]
    _, sources, tokens, part = parts.shape
    capacity = pick.shape[1]
    kinds = only.shape[1]
    return pl.pallas_call(
        weight_kernel,
        grid=(groups,),
        out_shape=jax.ShapeDtypeStruct((part, words), BF16),
        in_specs=[
            pl.BlockSpec((slots, part), lambda g: (0, 0)),
            pl.BlockSpec((sources, capacity, tokens), lambda g: (jnp.maximum(g - 1, 0), 0, 0)),
            pl.BlockSpec((1, sources, tokens, part), lambda g: (jnp.maximum(g - 1, 0), 0, 0, 0)),
            pl.BlockSpec((1, slots, packed.shape[2]), lambda g: (g, 0, 0)),
            pl.BlockSpec((slots, kinds), lambda g: (g, 0)),
        ],
        out_specs=pl.BlockSpec((part, words), lambda g: (0, 0)),
        scratch_shapes=[
            pltpu.VMEM((slots, part), BF16),
            pltpu.VMEM((part, slots), BF16),
            pltpu.VMEM((part, words), F32),
        ],
        compiler_params=pltpu.CompilerParams(dimension_semantics=("arbitrary",)),
        name="weight_product",
    )(own, pick, parts, packed, only)


def body(
    hidden,
    output_weight,
    owners,
    negatives,
    negative_mask,
    target_block,
    target_word,
    log_norm,
    cotangent,
):
    tokens, width = hidden.shape
    visits = owners.shape[1]
    per_own = negatives.shape[2]
    n_vocab = lax.axis_size("vocab")
    n_dp = lax.axis_size("dp")
    me = lax.axis_index("vocab")
    my_dp = lax.axis_index("dp")
    words = output_weight.shape[1]
    capacity = max(2, tokens * visits * 4 // (3 * n_vocab))
    slots = n_vocab * capacity
    part = width // n_dp

    facts = jnp.concatenate(
        [
            owners.T,
            negatives.reshape(tokens, -1).T,
            negative_mask.reshape(tokens, -1).T,
            target_block[None, :],
            target_word[None, :],
        ],
        axis=0,
    ).astype(BF16)
    facts = jnp.concatenate([facts, log_norm[None, :], cotangent[None, :]], axis=0)
    facts = jnp.pad(facts, ((0, -facts.shape[0] % 16), (0, 0)))
    blocks = n_dp * n_vocab

    cube = n_vocab == CUBE
    if cube:
        group_rows, part_rows, facts = front(hidden, facts, n_dp)
    else:
        group_rows = lax.all_gather(hidden, "vocab", axis=0, tiled=False)
        part_rows = lax.all_to_all(hidden, "dp", split_axis=1, concat_axis=0, tiled=True)
        part_rows = jnp.roll(part_rows.reshape(n_dp, tokens, part), -my_dp, axis=0)[1:]
        facts = lax.all_gather(lax.all_gather(facts, "dp", axis=0), "vocab", axis=0)
        facts = jnp.roll(facts, -my_dp, axis=1)
    part_rows = lax.all_gather(part_rows, "vocab", axis=1)
    facts = jnp.swapaxes(facts, 0, 1).reshape(blocks, -1, tokens)

    f = facts.astype(F32)
    pairs = visits * per_own
    hit = f[:, :visits, :] == me.astype(F32)
    neg = f[:, visits : visits + pairs, :]
    mask = f[:, visits + pairs : visits + 2 * pairs, :]
    base = visits + 2 * pairs
    t_block, t_word, norm, cot = (f[:, base + i, :] for i in range(4))
    named = jnp.any(hit, axis=1)
    cand = [jnp.where(hit[:, 0], t_block + 1.0, 0.0)]
    for n in range(per_own):
        value = jnp.zeros_like(t_block)
        for v in range(visits):
            i = v * per_own + n
            value = jnp.where(hit[:, v] & (mask[:, i] == 1.0), neg[:, i] + 1.0, value)
        cand.append(value)
    only = []
    for k, value in enumerate(cand):
        for earlier in cand[:k]:
            value = jnp.where(value == earlier, 0.0, value)
        only.append(value)
    upper = jnp.triu(jnp.ones((tokens, tokens), BF16), 1)
    rank = jnp.dot(named.astype(BF16), upper, preferred_element_type=F32)
    place = jnp.where(named, rank, -1.0)
    pick = (
        place[:, None, :] == jnp.arange(capacity, dtype=jnp.int32).astype(F32)[None, :, None]
    ).astype(BF16)
    attrs = jnp.stack(cand + only + [t_word, norm, cot], axis=1).astype(BF16)
    slot_facts = jnp.einsum("sct,sat->sca", pick, attrs, preferred_element_type=F32)
    kinds = per_own + 1
    all_only = slot_facts[:, :, kinds : 2 * kinds].reshape(n_dp * slots, kinds)
    mine = slot_facts[:n_vocab].reshape(slots, -1)
    my_pick = pick[:n_vocab]

    rows = jnp.einsum("sct,sth->sch", my_pick, group_rows, preferred_element_type=F32)
    rows = rows.astype(BF16).reshape(slots, width)
    scores = jnp.dot(rows, output_weight, preferred_element_type=F32)
    word_ids = jnp.arange(words, dtype=jnp.int32)[None, :]
    word_block = (word_ids // BLOCK + 1).astype(F32)
    word_in = (word_ids % BLOCK).astype(F32)
    counts = jnp.zeros((slots, words), F32)
    for k in range(kinds):
        counts = counts + jnp.where(mine[:, k : k + 1] == word_block, 1.0, 0.0)
    hot = jnp.where(
        (mine[:, 0:1] == word_block) & (mine[:, 2 * kinds : 2 * kinds + 1] == word_in), 1.0, 0.0
    )
    norm_col = mine[:, 2 * kinds + 1 : 2 * kinds + 2]
    cot_col = mine[:, 2 * kinds + 2 : 2 * kinds + 3]
    grown = jnp.where(counts > 0.0, counts * jnp.exp(scores - norm_col), 0.0)
    grad = (cot_col * (grown - hot)).astype(BF16)

    packed = []
    for k in range(kinds):
        which = mine[:, kinds + k : kinds + k + 1]
        value = jnp.zeros((slots, BLOCK), BF16)
        for b in range(BLK_DEV):
            value = jnp.where(which == b + 1.0, grad[:, b * BLOCK : (b + 1) * BLOCK], value)
        packed.append(value)
    packed = jnp.concatenate(packed, axis=1)
    back = lax.dot_general(
        grad, output_weight, (((1,), (1,)), ((), ())), preferred_element_type=F32
    ).astype(BF16)
    back = jnp.einsum(
        "sct,sch->sth", my_pick, back.reshape(n_vocab, capacity, width), preferred_element_type=F32
    ).astype(BF16)
    if cube:
        hidden_grad, packed = back_sum(back, packed, n_dp)
    else:
        hidden_grad = lax.psum_scatter(
            back.reshape(n_vocab * tokens, width), "vocab", scatter_dimension=0, tiled=True
        )
        packed = jnp.roll(lax.all_gather(packed, "dp", axis=0), -my_dp, axis=0)
    own_slots = lax.dynamic_slice_in_dim(rows, my_dp * part, part, 1)
    weight_grad = weight_product(own_slots, pick[n_vocab:], part_rows, packed, all_only, words)
    return (hidden_grad, weight_grad)


def solution(mesh):
    placed = (
        P(("dp", "vocab"), None),
        P(None, "vocab"),
        P(("dp", "vocab"), None),
        P(("dp", "vocab"), None, None),
        P(("dp", "vocab"), None, None),
        P(("dp", "vocab")),
        P(("dp", "vocab")),
        P(("dp", "vocab")),
        P(("dp", "vocab")),
    )
    return jax.shard_map(
        body,
        mesh=mesh,
        in_specs=placed,
        out_specs=(P(("dp", "vocab"), None), P("dp", "vocab")),
        check_vma=False,
    )
```
